32 devices in a mesh: groups: 2 (over y), tm: 8 (over z, x), height: 2 (over core).
Axes of the slice: x: 2, y: 2, z: 4, core: 2. Of those that a mesh axis runs over, the one named last changes fastest.
Arguments:
- video: bfloat16 [32, 8, 64, 256], P(('groups', 'tm'), 'height'), parts along dimension 0, may hold values from -6 to 6
- block_ids: int32 [32], P('groups'), parts along dimension 0, may hold values from 0 to 4, never falling along the last dimension, each value on 1 to 4 neighbouring positions
- conv_weight: bfloat16 [3, 3, 3, 256, 256], replicated, may hold values from -0.078125 to 0.078125
- w_query: bfloat16 [256, 256], replicated, may hold values from -4 to 4
- w_key: bfloat16 [256, 256], replicated, may hold values from -4 to 4
- w_value: bfloat16 [256, 256], replicated, may hold values from -0.375 to 0.375
- w_output: bfloat16 [256, 256], replicated, may hold values from -0.375 to 0.375
Outputs:
- encoded: bfloat16 [32, 8, 64, 256], P(('groups', 'tm'), 'height'), parts along dimension 0
The draws below stay inside these ranges and needn't reach their ends.
There are 2 independent parts, one for each index of `groups`. The reference program is written for one: setup_inputs(seed, part) draws one part's arguments, and reference() takes and returns one part's arrays. A program takes and returns all parts, laid end to end along the dimension named above; an argument that names none is the same for every part. Nothing has to cross between parts.
Inputs may be any that keep to these rules, and one draw needn't show every extreme that they name: `block_ids`: block ids never fall along the frames and start at 0; each block has 1 to 4 frames, and some block has exactly 4.
All inputs are finite; a program needn't handle non-finite values.
Results may differ from the reference program's by a relative error of at most 0.012.
Values may be sent and summed in bfloat16 or wider, within the bound.
A program may use at most 64 MiB of HBM per device.

```python
import math
import jax
import jax.numpy as jnp
import numpy as np
from jax import lax

C = 256
HD = 64
BLOCK = 4
WIDTH = 64
FRAMES = 16
ROWS = 8
BLOCKS = 5


def pair_weights(key):
    base_key, noise_key = jax.random.split(jax.random.fold_in(key, 11), 2)
    keys_part = jax.random.truncated_normal(base_key, -2.0, 2.0, (C, C), jnp.float32) * C ** (-0.5)
    other = jax.random.truncated_normal(noise_key, -2.0, 2.0, (C, C), jnp.float32) * C ** (-0.5)
    return (keys_part, other)


def draw_w_key(key, part):
    keys_part, other = pair_weights(key)
    return keys_part.astype(jnp.bfloat16)


def draw_w_query(key, part):
    keys_part, other = pair_weights(key)
    return other.astype(jnp.bfloat16)


def shard_levels(own_key, extent, pieces, low, high):
    def one(axis_at, shards_of):
        steps = jax.random.uniform(jax.random.fold_in(jax.random.fold_in(own_key, 6), axis_at), (shards_of,), jnp.float32, low / len(pieces), high / len(pieces))
        return jnp.repeat(jnp.exp(steps), extent[axis_at] // shards_of).reshape((-1,) + (1,) * (len(extent) - axis_at - 1))

    level = one(*pieces[0])
    for cut in pieces[1:]:
        level = level * one(*cut)
    return level


def length_profile(amount, total, bound, slope):
    loads = [(1 << 20) // math.isqrt(grade ** slope) + 1 for grade in range(2, amount + 1)]
    rest, counts = total - bound - (amount - 1), [1] * (amount - 1)
    while rest > 0:
        free = [i for i in range(amount - 1) if counts[i] < bound]
        pool, budget = sum([loads[i] for i in free]), rest
        for i in free:
            addition = min(bound - counts[i], max(1, budget * loads[i] // pool), rest)
            counts[i] = counts[i] + addition
            rest = rest - addition
    return np.array([bound] + counts)


def ragged(stream_key, count, total, bound, lean):
    if count == 2:
        one = jax.random.randint(stream_key, (), max(1, total - bound), min(bound, total - 1) + 1)
        return jnp.stack([one, total - one])
    sizes = jnp.asarray(length_profile(count, total, bound, lean), jnp.int32)
    couples = (count - 1) // 2
    giver, receiver = sizes[1:1 + 2 * couples:2], sizes[2:2 + 2 * couples:2]
    slack = jnp.minimum(giver - 1, bound - receiver)
    moved = jax.random.randint(jax.random.fold_in(stream_key, 1), (couples,), 0, 1 << 20) % (slack + 1)
    sizes = sizes.at[1:1 + 2 * couples:2].set(giver - moved).at[2:2 + 2 * couples:2].set(receiver + moved)
    return sizes[jax.random.permutation(jax.random.fold_in(stream_key, 2), count)]


def gaussian(own_key, dims, spread, most, cuts=(), held_as=jnp.bfloat16):
    loudness = shard_levels(own_key, dims, cuts, -0.22, 0.18) if cuts else 1.0
    entries = jax.random.normal(own_key, dims, jnp.float32) * spread * loudness
    return jnp.minimum(jnp.maximum(entries, -most), most).astype(held_as)


def setup_inputs(seed: int = 0, part: int = 0) -> dict:
    splits = jax.random.split(jax.random.key(seed), 8)
    own_keys = jax.random.split(jax.random.fold_in(splits[7], part), 8)
    video = gaussian(own_keys[0], (FRAMES, ROWS, WIDTH, C), 1.0, 6.0, ((0, 8), (1, 2)))
    block_ids = jnp.searchsorted(jnp.cumsum(ragged(own_keys[1], BLOCKS, FRAMES, BLOCK, 1)), jnp.arange(FRAMES), side="right").astype(jnp.int32)
    conv_weight = gaussian(splits[2], (3, 3, 3, C, C), (27 * C) ** -0.5, 0.078125)
    w_query = draw_w_query(jax.random.fold_in(splits[7], 71), part)
    w_key = draw_w_key(jax.random.fold_in(splits[7], 71), part)
    w_value = gaussian(splits[5], (C, C), C ** -0.5, 0.375)
    w_output = gaussian(splits[6], (C, C), C ** -0.5, 0.375)
    return dict(video=video, block_ids=block_ids, conv_weight=conv_weight, w_query=w_query, w_key=w_key, w_value=w_value, w_output=w_output)


def normalize(values):
    wide = values.astype(jnp.float32)
    return wide * lax.rsqrt(lax.optimization_barrier(jnp.mean(wide * wide, axis=-1, keepdims=True)) + 1e-06)

def project(flat, weight):
    return jnp.dot(flat, weight, preferred_element_type=jnp.float32).astype(jnp.bfloat16)

def reference(video, block_ids, conv_weight, w_query, w_key, w_value, w_output):
    frames, rows, cols, chans = video.shape
    heads = chans // HD
    activated = jax.nn.silu(normalize(video)).astype(jnp.bfloat16)
    padded = jnp.pad(activated, ((2, 0), (1, 1), (1, 1), (0, 0)))
    total = jnp.zeros((frames * rows * cols, chans), jnp.float32)
    for tap_t in range(3):
        for tap_r in range(3):
            for tap_w in range(3):
                window = padded[tap_t:tap_t + frames, tap_r:tap_r + rows, tap_w:tap_w + cols].reshape(-1, chans)
                total = total + jnp.dot(window, conv_weight[tap_t, tap_r, tap_w], preferred_element_type=jnp.float32)
    hidden = (video.astype(jnp.float32) + total.reshape(video.shape)).astype(jnp.bfloat16)
    normed = normalize(hidden).astype(jnp.bfloat16).reshape(-1, chans)
    query = project(normed, w_query).reshape(frames, rows, cols, heads, HD)
    keys = project(normed, w_key).reshape(frames, rows, cols, heads, HD)
    values = project(normed, w_value).reshape(frames, rows, cols, heads, HD)
    order = jnp.arange(frames, dtype=jnp.int32)
    allowed = (order[None, :] <= order[:, None]) & (block_ids[None, :] >= block_ids[:, None] - 1)

    def one_row(packed):
        q_row, k_row, v_row = packed
        scores = jnp.einsum('fwhd,kwhd->whfk', q_row.astype(jnp.float32), k_row.astype(jnp.float32)) * HD ** (-0.5)
        scores = jnp.where(allowed[None, None], scores, -1e+30)
        top = lax.optimization_barrier(jnp.max(scores, axis=-1, keepdims=True))
        expo = jnp.exp(scores - top)
        weights = (expo / lax.optimization_barrier(jnp.sum(expo, axis=-1, keepdims=True))).astype(jnp.bfloat16)
        out = jnp.einsum('whfk,kwhd->fwhd', weights.astype(jnp.float32), v_row.astype(jnp.float32))
        return out.astype(jnp.bfloat16)
    attended = lax.map(one_row, (jnp.moveaxis(query, 1, 0), jnp.moveaxis(keys, 1, 0), jnp.moveaxis(values, 1, 0)))
    attended = jnp.moveaxis(attended, 0, 1).reshape(-1, chans)
    mixed = hidden.astype(jnp.float32).reshape(-1, chans) + jnp.dot(attended, w_output, preferred_element_type=jnp.float32)
    return mixed.astype(jnp.bfloat16).reshape(video.shape)
```

```python
import functools

import jax
import jax.numpy as jnp
from jax import lax
from jax.experimental import pallas as pl
from jax.experimental.pallas import tpu as pltpu
from jax.sharding import PartitionSpec as P

HD = 64
REACH = 7
MESH = pl.DeviceIdType.MESH


def normalize(wide):
    return wide * lax.rsqrt(jnp.mean(wide * wide, axis=-1, keepdims=True) + 1e-06)


def kernel(n, parts, ids, video, conv_w, w_q, w_k, w_v, w_o, out,
           raw, act, cw, pw, acc, held, nb, qs, ks, vs, place, spread,
           load_sem, weight_sem, row_send, row_recv, halo_send, halo_recv,
           own_send, fwd_send, nb_recv):
    count, rows, cols, chans = video.shape
    pix = rows * cols
    heads = chans // HD
    me = lax.axis_index("tm")
    core = lax.axis_index("height")
    even = lax.rem(me, 2) == 0
    odd = lax.rem(me, 2) == 1
    chunk = pix // parts

    def peer(by):
        return {"tm": me + by}

    other = {"height": 1 - core}

    own_load = pltpu.make_async_copy(video, raw.at[2:4, 1:rows + 1], load_sem)
    own_load.start()
    w_loads = {}
    for a in (2, 1, 0):
        w_loads[a] = pltpu.make_async_copy(conv_w.at[a], cw.at[a], weight_sem.at[a])
        w_loads[a].start()
    p_loads = []
    for j, w in enumerate((w_q, w_k, w_v, w_o)):
        p_loads.append(pltpu.make_async_copy(w, pw.at[j], weight_sem.at[3 + j]))
        p_loads[-1].start()

    barrier = pltpu.get_barrier_semaphore()
    near = [(me >= 1, -1), (me <= n - 2, 1), (me >= 2, -2), (me <= n - 3, 2)]
    pl.semaphore_signal(barrier, inc=1, device_id=other, device_id_type=MESH)
    for cond, by in near:
        @pl.when(cond)
        def _(by=by):
            pl.semaphore_signal(barrier, inc=1, device_id=peer(by), device_id_type=MESH)

    blank = jnp.zeros((cols, chans), jnp.bfloat16)
    outer = (rows + 1) * core
    inner = (rows + 1) * (1 - core)
    for e in range(4):
        raw[e, outer] = blank

    @pl.when(me == 0)
    def _():
        for e in range(2):
            for r in range(rows + 2):
                raw[e, r] = blank

    for d in range(1, 5):
        @pl.when(me < d)
        def _(d=d):
            for f in range(2):
                nb[8 - 2 * d + f] = jnp.zeros((pix, chans), jnp.bfloat16)

    for at in (0, 1, n - 2, n - 1):
        @pl.when(me == at)
        def _(at=at):
            pl.semaphore_wait(barrier, 1 + sum(0 <= at + by < n for by in (-2, -1, 1, 2)))

    @pl.when((me >= 2) & (me <= n - 3))
    def _():
        pl.semaphore_wait(barrier, 5)

    edge = (rows - 1) * (1 - core)
    landing = (rows + 1) * core

    def halo(f):
        return pltpu.make_async_remote_copy(
            src_ref=video.at[f], dst_ref=raw.at[f, 1:rows + 1],
            send_sem=halo_send.at[f], recv_sem=halo_recv.at[f],
            device_id=peer(1), device_id_type=MESH)

    def row(e):
        src = video.at[e - 2, edge] if e >= 2 else raw.at[e, 1 + edge]
        return pltpu.make_async_remote_copy(
            src_ref=src, dst_ref=raw.at[e, landing],
            send_sem=row_send.at[e], recv_sem=row_recv.at[e],
            device_id=other, device_id_type=MESH)

    @pl.when(me <= n - 2)
    def _():
        halo(1).start()
        halo(0).start()

    row(2).start()
    row(3).start()

    for f in range(2):
        for s in range(f, f + 8):
            c0 = lax.broadcasted_iota(jnp.int32, (chans, 128), 0) // HD
            l0 = lax.broadcasted_iota(jnp.int32, (chans, 128), 1)
            place[f * 8 + s - f] = jnp.where(
                l0 == c0 + (s * 8 + f * 4), HD ** (-0.5), 0.0).astype(jnp.bfloat16)
            c1 = lax.broadcasted_iota(jnp.int32, (128, chans), 1) // HD
            l1 = lax.broadcasted_iota(jnp.int32, (128, chans), 0)
            spread[f * 8 + s - f] = jnp.where(
                l1 == c1 + (s * 8 + f * 4), 1.0, 0.0).astype(jnp.bfloat16)

    col = lax.broadcasted_iota(jnp.int32, (cols, chans), 0)

    def activate(e, r):
        v = normalize(raw[e, r].astype(jnp.float32))
        v = v / (1.0 + jnp.exp(-v))
        act[e, r, :, chans:2 * chans] = v.astype(jnp.bfloat16)
        left = jnp.where(col == 0, 0.0, pltpu.roll(v, 1, 0))
        right = jnp.where(col == cols - 1, 0.0, pltpu.roll(v, cols - 1, 0))
        act[e, r, :, 0:chans] = left.astype(jnp.bfloat16)
        act[e, r, :, 2 * chans:3 * chans] = right.astype(jnp.bfloat16)

    def activate_inside(e):
        def step(r, carry):
            activate(e, r)
            return carry
        lax.fori_loop(1, rows + 1, step, 0)
        activate(e, outer)

    def taps(f, a):
        total = None
        for b in range(3):
            window = act[f + a, b:b + rows].reshape(pix, 3 * chans)
            term = jnp.dot(window, cw[a, b], preferred_element_type=jnp.float32)
            total = term if total is None else total + term
        return total

    own_load.wait()
    activate_inside(2)
    activate_inside(3)
    row(2).wait()
    activate(2, inner)
    row(3).wait()
    activate(3, inner)
    w_loads[2].wait()
    acc[0] = taps(0, 2)
    acc[1] = taps(1, 2)
    w_loads[1].wait()
    acc[1] += taps(1, 1)

    def arrive(e):
        @pl.when(me >= 1)
        def _():
            halo(e).wait_recv()
            row(e).start()
        activate_inside(e)

        @pl.when(me >= 1)
        def _():
            row(e).wait()
        activate(e, inner)

    def copy_to(idx_src, idx_dst, q, by, send_sem):
        cut = pl.ds(q * chunk, chunk)
        return pltpu.make_async_remote_copy(
            src_ref=nb.at[idx_src, cut], dst_ref=nb.at[idx_dst, cut],
            send_sem=send_sem, recv_sem=nb_recv.at[idx_dst, q],
            device_id=peer(by), device_id_type=MESH)

    def own_next(f, q):
        return copy_to(8 + f, 6 + f, q, 1, own_send.at[0, f, q])

    def own_skip(f, q):
        return copy_to(8 + f, 4 + f, q, 2, own_send.at[1, f, q])

    def finish(f):
        mixed = raw[2 + f, 1:rows + 1].reshape(pix, chans).astype(jnp.float32) + acc[f]
        hidden = mixed.astype(jnp.bfloat16)
        held[f] = hidden
        nb[8 + f] = normalize(hidden.astype(jnp.float32)).astype(jnp.bfloat16)

        @pl.when(me <= n - 3)
        def _():
            for q in range(parts):
                own_skip(f, q).start()

        @pl.when(even)
        def _():
            for q in range(parts):
                own_next(f, q).start()

    arrive(1)
    w_loads[0].wait()
    acc[1] += taps(1, 0)
    finish(1)
    acc[0] += taps(0, 1)
    arrive(0)
    acc[0] += taps(0, 0)
    finish(0)

    for load in p_loads:
        load.wait()

    def keyed(idx):
        x = nb[idx]
        ks[idx] = jnp.dot(x, pw[1], preferred_element_type=jnp.float32).astype(jnp.bfloat16)
        vs[idx] = jnp.dot(x, pw[2], preferred_element_type=jnp.float32).astype(jnp.bfloat16)

    for f in (1, 0):
        qs[f] = jnp.dot(nb[8 + f], pw[0], preferred_element_type=jnp.float32).astype(jnp.bfloat16)
        keyed(8 + f)

    def fwd_side_even(f, q):
        return copy_to(4 + f, 2 + f, q, 1, fwd_send.at[0, f, q])

    def fwd_side_odd(f, q):
        return copy_to(4 + f, 6 + f, q, -1, fwd_send.at[0, f, q])

    def fwd_skip(f, q):
        return copy_to(4 + f, f, q, 2, fwd_send.at[1, f, q])

    def fwd_far_odd(f, q):
        return copy_to(f, 2 + f, q, -1, fwd_send.at[2, f, q])

    def landed(idx, q):
        copy_to(idx, idx, q, 0, own_send.at[0, 0, 0]).wait_recv()

    for f in (1, 0):
        for q in range(parts):
            @pl.when(even & (me >= 2))
            def _(f=f, q=q):
                landed(4 + f, q)
                fwd_side_even(f, q).start()

            if f == 1:
                @pl.when(even & (me >= 2) & (me <= n - 3))
                def _(f=f, q=q):
                    fwd_skip(f, q).start()

            @pl.when(odd & (me >= 2))
            def _(f=f, q=q):
                landed(4 + f, q)
                fwd_side_odd(f, q).start()

            @pl.when(odd & (me >= 2) & (me <= n - 3))
            def _(f=f, q=q):
                fwd_skip(f, q).start()
        keyed(4 + f)

    for f in (1, 0):
        for q in range(parts):
            @pl.when(odd & (me >= 4))
            def _(f=f, q=q):
                landed(f, q)
                fwd_far_odd(f, q).start()

            if f == 1:
                @pl.when(even & (me >= 4))
                def _(f=f, q=q):
                    landed(f, q)
        if f == 1:
            keyed(1)

    for d in (1, 3):
        for f in (1, 0):
            @pl.when(me >= d)
            def _(d=d, f=f):
                for q in range(parts):
                    landed(8 - 2 * d + f, q)
            keyed(8 - 2 * d + f)

    frames = ids.shape[0]
    lane = lax.broadcasted_iota(jnp.int32, (1, 128), 1)
    slot = lane // 8
    which = lax.rem(lane, 8) // 4
    first = me * 2
    local_first = first
    key_id = jnp.zeros((1, 128), jnp.int32)
    for s in range(9):
        at = lax.rem(local_first - REACH + s + frames, frames)
        key_id = jnp.where(slot == s, ids[at], key_id)
    query_id = jnp.where(which == 0, ids[local_first], ids[local_first + 1])
    key_frame = first - REACH + slot
    allowed = ((slot < 9) & (key_frame >= 0) & (key_frame <= first + which)
               & (slot >= which) & (slot < which + 8) & (key_id >= query_id - 1))

    scores = jnp.zeros((pix, 128), jnp.float32)
    for f in range(2):
        query = qs[f].astype(jnp.float32)
        for j in range(8):
            prod = query * ks[1 + f + j].astype(jnp.float32)
            high = prod.astype(jnp.bfloat16)
            low = (prod - high.astype(jnp.float32)).astype(jnp.bfloat16)
            spot = place[f * 8 + j]
            scores = scores + jnp.dot(high, spot, preferred_element_type=jnp.float32)
            scores = scores + jnp.dot(low, spot, preferred_element_type=jnp.float32)
    scores = jnp.where(allowed, scores, -1e30)
    top = scores
    for by in (64, 32, 16, 8):
        top = jnp.maximum(top, pltpu.roll(top, by, 1))
    expo = jnp.exp(scores - top)
    total = expo
    for by in (64, 32, 16, 8):
        total = total + pltpu.roll(total, by, 1)
    weights = (expo / total).astype(jnp.bfloat16)
    for f in range(2):
        got = jnp.zeros((pix, chans), jnp.float32)
        for j in range(8):
            wide = jnp.dot(weights, spread[f * 8 + j], preferred_element_type=jnp.float32)
            got = got + wide * vs[1 + f + j].astype(jnp.float32)
        mixed = held[f].astype(jnp.float32) + jnp.dot(
            got.astype(jnp.bfloat16), pw[3], preferred_element_type=jnp.float32)
        out[f] = mixed.astype(jnp.bfloat16).reshape(rows, cols, chans)

    @pl.when(me <= n - 2)
    def _():
        halo(1).wait_send()
        halo(0).wait_send()

    for f in range(2):
        for q in range(parts):
            @pl.when(me <= n - 3)
            def _(f=f, q=q):
                own_skip(f, q).wait_send()

            @pl.when(even)
            def _(f=f, q=q):
                own_next(f, q).wait_send()

            @pl.when(me >= 2)
            def _(f=f, q=q):
                fwd_side_even(f, q).wait_send()

            if f == 1:
                @pl.when(even & (me >= 2) & (me <= n - 3))
                def _(f=f, q=q):
                    fwd_skip(f, q).wait_send()

            @pl.when(odd & (me >= 2) & (me <= n - 3))
            def _(f=f, q=q):
                fwd_skip(f, q).wait_send()

            @pl.when(odd & (me >= 4))
            def _(f=f, q=q):
                fwd_far_odd(f, q).wait_send()


def per_device(video, block_ids, conv_weight, w_query, w_key, w_value, w_output):
    count, rows, cols, chans = video.shape
    n = lax.axis_size("tm")
    assert count == 2 and n % 2 == 0 and n >= 4 and lax.axis_size("height") == 2
    pix = rows * cols
    parts = 2
    bf = jnp.bfloat16
    anywhere = pl.BlockSpec(memory_space=pl.ANY)
    return pl.pallas_call(
        functools.partial(kernel, n, parts),
        out_shape=jax.ShapeDtypeStruct(video.shape, bf),
        in_specs=[pl.BlockSpec(memory_space=pltpu.SMEM)] + [anywhere] * 6,
        out_specs=pl.BlockSpec(memory_space=pltpu.VMEM),
        scratch_shapes=[
            pltpu.VMEM((4, rows + 2, cols, chans), bf),
            pltpu.VMEM((4, rows + 2, cols, 3 * chans), bf),
            pltpu.VMEM((3, 3, 3 * chans, chans), bf),
            pltpu.VMEM((4, chans, chans), bf),
            pltpu.VMEM((2, pix, chans), jnp.float32),
            pltpu.VMEM((2, pix, chans), bf),
            pltpu.VMEM((10, pix, chans), bf),
            pltpu.VMEM((2, pix, chans), bf),
            pltpu.VMEM((10, pix, chans), bf),
            pltpu.VMEM((10, pix, chans), bf),
            pltpu.VMEM((16, chans, 128), bf),
            pltpu.VMEM((16, 128, chans), bf),
            pltpu.SemaphoreType.DMA,
            pltpu.SemaphoreType.DMA((7,)),
            pltpu.SemaphoreType.DMA((4,)),
            pltpu.SemaphoreType.DMA((4,)),
            pltpu.SemaphoreType.DMA((2,)),
            pltpu.SemaphoreType.DMA((2,)),
            pltpu.SemaphoreType.DMA((2, 2, parts)),
            pltpu.SemaphoreType.DMA((3, 2, parts)),
            pltpu.SemaphoreType.DMA((10, parts)),
        ],
        compiler_params=pltpu.CompilerParams(collective_id=0, has_side_effects=True),
    )(block_ids, video, conv_weight.reshape(3, 3, 3 * chans, chans), w_query, w_key, w_value, w_output)


def solution(mesh):
    placed = (P(("groups", "tm"), "height", None, None), P("groups"), P(), P(), P(), P(), P())
    return jax.shard_map(
        per_device,
        mesh=mesh,
        in_specs=placed,
        out_specs=P(("groups", "tm"), "height", None, None),
        check_vma=False,
    )
```

```python
import functools

import jax
import jax.numpy as jnp
from jax import lax
from jax.experimental import pallas as pl
from jax.experimental.pallas import tpu as pltpu
from jax.sharding import PartitionSpec as P

HD = 64
REACH = 7
MESH = pl.DeviceIdType.MESH


def normalize(wide):
    return wide * lax.rsqrt(jnp.mean(wide * wide, axis=-1, keepdims=True) + 1e-06)


def kernel(n, ids, video, conv_w, w_q, w_k, w_v, out, held,
           raw, act, cw, pw, acc, nb, qs, ks, vs, place, spread,
           load_sem, weight_sem, row_send, row_recv, halo_send, halo_recv,
           own_send, fwd_send, nb_recv):
    count, rows, cols, chans = video.shape
    me = lax.axis_index("tm")
    core = lax.axis_index("height")
    even = lax.rem(me, 2) == 0
    odd = lax.rem(me, 2) == 1

    def peer(by):
        return {"tm": me + by}

    other = {"height": 1 - core}

    own_load = pltpu.make_async_copy(video, raw.at[2:4, 1:rows + 1], load_sem)
    own_load.start()
    w_loads = {}
    for a in (2, 1, 0):
        w_loads[a] = pltpu.make_async_copy(conv_w.at[a], cw.at[a], weight_sem.at[a])
        w_loads[a].start()
    p_loads = []
    for j, w in enumerate((w_q, w_k, w_v)):
        p_loads.append(pltpu.make_async_copy(w, pw.at[j], weight_sem.at[3 + j]))
        p_loads[-1].start()

    barrier = pltpu.get_barrier_semaphore()
    near = [(me >= 1, -1), (me <= n - 2, 1), (me >= 2, -2), (me <= n - 3, 2)]
    pl.semaphore_signal(barrier, inc=1, device_id=other, device_id_type=MESH)
    for cond, by in near:
        @pl.when(cond)
        def _(by=by):
            pl.semaphore_signal(barrier, inc=1, device_id=peer(by), device_id_type=MESH)

    blank = jnp.zeros((cols, chans), jnp.bfloat16)
    outer = (rows + 1) * core
    inner = (rows + 1) * (1 - core)
    for e in range(4):
        raw[e, outer] = blank

    @pl.when(me == 0)
    def _():
        for e in range(2):
            for r in range(rows + 2):
                raw[e, r] = blank

    for d in range(1, 5):
        @pl.when(me < d)
        def _(d=d):
            for f in range(2):
                nb[8 - 2 * d + f] = jnp.zeros((rows, cols, chans), jnp.bfloat16)

    for at in (0, 1, n - 2, n - 1):
        @pl.when(me == at)
        def _(at=at):
            pl.semaphore_wait(barrier, 1 + sum(0 <= at + by < n for by in (-2, -1, 1, 2)))

    @pl.when((me >= 2) & (me <= n - 3))
    def _():
        pl.semaphore_wait(barrier, 5)

    edge = (rows - 1) * (1 - core)
    landing = (rows + 1) * core
    half = rows // 2

    def halo(part):
        start, size = ((core, rows - 1), (edge, 1))[part]
        return pltpu.make_async_remote_copy(
            src_ref=video.at[:, pl.ds(start, size)],
            dst_ref=raw.at[0:2, pl.ds(1 + start, size)],
            send_sem=halo_send.at[part], recv_sem=halo_recv.at[part],
            device_id=peer(1), device_id_type=MESH)

    def row(e):
        src = video.at[:, edge] if e else raw.at[0:2, 1 + edge]
        return pltpu.make_async_remote_copy(
            src_ref=src, dst_ref=raw.at[2 * e:2 * e + 2, landing],
            send_sem=row_send.at[e], recv_sem=row_recv.at[e],
            device_id=other, device_id_type=MESH)

    @pl.when(me <= n - 2)
    def _():
        halo(0).start()
        halo(1).start()

    row(1).start()

    col = lax.broadcasted_iota(jnp.int32, (cols, chans), 0)

    def activate(e, r):
        v = normalize(raw[e, r].astype(jnp.float32))
        v = v / (1.0 + jnp.exp(-v))
        act[e, r, :, chans:2 * chans] = v.astype(jnp.bfloat16)
        left = jnp.where(col == 0, 0.0, pltpu.roll(v, 1, 0))
        right = jnp.where(col == cols - 1, 0.0, pltpu.roll(v, cols - 1, 0))
        act[e, r, :, 0:chans] = left.astype(jnp.bfloat16)
        act[e, r, :, 2 * chans:3 * chans] = right.astype(jnp.bfloat16)

    def activate_rows(e0, start, size):
        for e in (e0, e0 + 1):
            for r in range(size):
                activate(e, start + r)

    empty = jnp.zeros((cols, 3 * chans), jnp.bfloat16)
    for e in range(4):
        act[e, outer] = empty

    def taps(p, a):
        base = half * (p + core * (1 - 2 * p))
        total = None
        for b in range(3):
            window = act[a:a + 2, pl.ds(base + b, half)].reshape(2 * half * cols, 3 * chans)
            term = jnp.dot(window, cw[a, b], preferred_element_type=jnp.float32)
            total = term if total is None else total + term
        return total

    own_load.wait()
    activate_rows(2, 1, rows)
    w_loads[2].wait()
    acc[0] = taps(0, 2)
    row(1).wait()
    activate_rows(2, inner, 1)
    acc[1] = taps(1, 2)
    w_loads[1].wait()
    w_loads[0].wait()

    def line(p):
        return p + core * (rows - 1 - 2 * p)

    def copy_to(src, dst, size, p, by, send_sem, recv_sem):
        return pltpu.make_async_remote_copy(
            src_ref=nb.at[src:src + size, line(p)], dst_ref=nb.at[dst:dst + size, line(p)],
            send_sem=send_sem, recv_sem=recv_sem,
            device_id=peer(by), device_id_type=MESH)

    def own_next(p):
        return copy_to(8, 6, 2, p, 1, own_send.at[0, p], nb_recv.at[0, p])

    def own_skip(p):
        return copy_to(8, 4, 2, p, 2, own_send.at[1, p], nb_recv.at[1, p])

    def fwd_side_even(p):
        return copy_to(4, 2, 2, p, 1, fwd_send.at[0, p], nb_recv.at[2, p])

    def fwd_side_odd(p):
        return copy_to(4, 6, 2, p, -1, fwd_send.at[0, p], nb_recv.at[0, p])

    def fwd_skip_even(p):
        return copy_to(5, 1, 1, p, 2, fwd_send.at[1, p], nb_recv.at[3, p])

    def fwd_skip_odd(p):
        return copy_to(4, 0, 2, p, 2, fwd_send.at[1, p], nb_recv.at[3, p])

    def fwd_far_odd(p):
        return copy_to(0, 2, 2, p, -1, fwd_send.at[2, p], nb_recv.at[2, p])

    def first_line(p):
        return half * (p + core * (1 - 2 * p))

    def finish(p):
        at = pl.ds(first_line(p), half)
        mixed = raw[2:4, pl.ds(first_line(p) + 1, half)].astype(jnp.float32)
        mixed = mixed + acc[p].reshape(mixed.shape)
        hidden = mixed.astype(jnp.bfloat16)
        held[:, at] = hidden
        nb[8:10, at] = normalize(hidden.astype(jnp.float32)).astype(jnp.bfloat16)
        for k in range(half):
            @pl.when(me <= n - 3)
            def _(k=k):
                own_skip(half * p + k).start()

            @pl.when(even)
            def _(k=k):
                own_next(half * p + k).start()

    @pl.when(me >= 1)
    def _():
        halo(0).wait_recv()
    activate_rows(0, 1 + core, rows - 1)
    acc[0] += taps(0, 1) + taps(0, 0)
    finish(0)

    @pl.when(me >= 1)
    def _():
        halo(1).wait_recv()
        row(0).start()
    activate_rows(0, 1 + edge, 1)

    @pl.when(me >= 1)
    def _():
        row(0).wait()
    activate_rows(0, inner, 1)
    acc[1] += taps(1, 1) + taps(1, 0)
    finish(1)

    c0 = lax.broadcasted_iota(jnp.int32, (chans, 128), 0) // HD
    l0 = lax.broadcasted_iota(jnp.int32, (chans, 128), 1)
    c1 = lax.broadcasted_iota(jnp.int32, (128, chans), 1) // HD
    l1 = lax.broadcasted_iota(jnp.int32, (128, chans), 0)
    for f in range(2):
        for s in range(f, f + 8):
            place[f * 8 + s - f] = jnp.where(
                l0 == c0 + (s * 8 + f * 4), HD ** (-0.5), 0.0).astype(jnp.bfloat16)
            spread[f * 8 + s - f] = jnp.where(
                l1 == c1 + (s * 8 + f * 4), 1.0, 0.0).astype(jnp.bfloat16)

    for load in p_loads:
        load.wait()

    def project(x, j):
        return jnp.dot(x, pw[j], preferred_element_type=jnp.float32).astype(jnp.bfloat16)

    def keyed(idx, size, p):
        at = pl.ds(first_line(p), half)
        shape = (size, half, cols, chans)
        x = nb[idx:idx + size, at].reshape(size * half * cols, chans)
        ks[idx:idx + size, at] = project(x, 1).reshape(shape)
        vs[idx:idx + size, at] = project(x, 2).reshape(shape)

    for p in range(2):
        at = pl.ds(first_line(p), half)
        x = nb[8:10, at].reshape(2 * half * cols, chans)
        qs[:, at] = project(x, 0).reshape(2, half, cols, chans)
        keyed(8, 2, p)

    def relay_near(p):
        @pl.when(even & (me >= 2))
        def _():
            own_skip(p).wait_recv()
            fwd_side_even(p).start()

        @pl.when(even & (me >= 2) & (me <= n - 3))
        def _():
            fwd_skip_even(p).start()

        @pl.when(odd & (me >= 2))
        def _():
            own_skip(p).wait_recv()
            fwd_side_odd(p).start()

        @pl.when(odd & (me >= 2) & (me <= n - 3))
        def _():
            fwd_skip_odd(p).start()

    def relay_far(p):
        @pl.when(odd & (me >= 4))
        def _():
            fwd_skip_odd(p).wait_recv()
            fwd_far_odd(p).start()

        @pl.when(even & (me >= 4))
        def _():
            fwd_skip_even(p).wait_recv()

    frames = ids.shape[0]
    lane = lax.broadcasted_iota(jnp.int32, (1, 128), 1)
    slot = lane // 8
    which = lax.rem(lane, 8) // 4
    first = me * 2
    key_id = jnp.zeros((1, 128), jnp.int32)
    for s in range(9):
        key_id = jnp.where(slot == s, ids[lax.rem(first - REACH + s + frames, frames)], key_id)
    query_id = jnp.where(which == 0, ids[first], ids[first + 1])
    key_frame = first - REACH + slot
    allowed = ((slot < 9) & (key_frame >= 0) & (key_frame <= first + which)
               & (slot >= which) & (slot < which + 8) & (key_id >= query_id - 1))

    def attend(p):
        at = pl.ds(first_line(p), half)
        group = half * cols

        def part(ref, idx):
            return ref[idx, at].reshape(group, chans).astype(jnp.float32)

        scores = jnp.zeros((group, 128), jnp.float32)
        for f in range(2):
            query = part(qs, f)
            for j in range(8):
                prod = query * part(ks, 1 + f + j)
                high = prod.astype(jnp.bfloat16)
                low = (prod - high.astype(jnp.float32)).astype(jnp.bfloat16)
                spot = place[f * 8 + j]
                scores = scores + jnp.dot(high, spot, preferred_element_type=jnp.float32)
                scores = scores + jnp.dot(low, spot, preferred_element_type=jnp.float32)
        scores = jnp.where(allowed, scores, -1e30)
        top = scores
        for by in (64, 32, 16, 8):
            top = jnp.maximum(top, pltpu.roll(top, by, 1))
        expo = jnp.exp(scores - top)
        total = expo
        for by in (64, 32, 16, 8):
            total = total + pltpu.roll(total, by, 1)
        weights = (expo / total).astype(jnp.bfloat16)
        for f in range(2):
            got = jnp.zeros((group, chans), jnp.float32)
            for j in range(8):
                wide = jnp.dot(weights, spread[f * 8 + j], preferred_element_type=jnp.float32)
                got = got + wide * part(vs, 1 + f + j)
            out[f, at] = got.astype(jnp.bfloat16).reshape(half, cols, chans)

    def take(d, p):
        sem = nb_recv.at[{1: 0, 3: 2}[d], p]

        @pl.when(me >= d)
        def _():
            copy_to(8 - 2 * d, 8 - 2 * d, 2, p, 1, own_send.at[0, 0], sem).wait_recv()

    for p in range(half):
        relay_near(p)
    keyed(4, 2, 0)
    for p in range(half, rows):
        relay_near(p)
    keyed(4, 2, 1)
    for p in range(half):
        relay_far(p)
    keyed(1, 1, 0)
    for p in range(half):
        take(1, p)
    keyed(6, 2, 0)
    relay_far(half)
    for p in range(half):
        take(3, p)
    keyed(2, 2, 0)
    attend(0)
    for p in range(half + 1, rows):
        relay_far(p)
    keyed(1, 1, 1)
    for p in range(half, rows):
        take(1, p)
    keyed(6, 2, 1)
    for p in range(half, rows):
        take(3, p)
    keyed(2, 2, 1)
    attend(1)

    @pl.when(me <= n - 2)
    def _():
        halo(0).wait_send()
        halo(1).wait_send()

    for p in range(rows):
        @pl.when(me <= n - 3)
        def _(p=p):
            own_skip(p).wait_send()

        @pl.when(even)
        def _(p=p):
            own_next(p).wait_send()

        @pl.when(me >= 2)
        def _(p=p):
            fwd_side_even(p).wait_send()

        @pl.when(even & (me >= 2) & (me <= n - 3))
        def _(p=p):
            fwd_skip_even(p).wait_send()

        @pl.when(odd & (me >= 2) & (me <= n - 3))
        def _(p=p):
            fwd_skip_odd(p).wait_send()

        @pl.when(odd & (me >= 4))
        def _(p=p):
            fwd_far_odd(p).wait_send()


def per_device(video, block_ids, conv_weight, w_query, w_key, w_value, w_output):
    count, rows, cols, chans = video.shape
    n = lax.axis_size("tm")
    assert count == 2 and n % 2 == 0 and n >= 4 and lax.axis_size("height") == 2
    assert rows % 2 == 0
    group = rows * cols
    bf = jnp.bfloat16
    anywhere = pl.BlockSpec(memory_space=pl.ANY)
    attended, hidden = pl.pallas_call(
        functools.partial(kernel, n),
        out_shape=[jax.ShapeDtypeStruct(video.shape, bf)] * 2,
        in_specs=[pl.BlockSpec(memory_space=pltpu.SMEM)] + [anywhere] * 5,
        out_specs=[pl.BlockSpec(memory_space=pltpu.VMEM)] * 2,
        scratch_shapes=[
            pltpu.VMEM((4, rows + 2, cols, chans), bf),
            pltpu.VMEM((4, rows + 2, cols, 3 * chans), bf),
            pltpu.VMEM((3, 3, 3 * chans, chans), bf),
            pltpu.VMEM((3, chans, chans), bf),
            pltpu.VMEM((2, group, chans), jnp.float32),
            pltpu.VMEM((10, rows, cols, chans), bf),
            pltpu.VMEM((2, rows, cols, chans), bf),
            pltpu.VMEM((10, rows, cols, chans), bf),
            pltpu.VMEM((10, rows, cols, chans), bf),
            pltpu.VMEM((16, chans, 128), bf),
            pltpu.VMEM((16, 128, chans), bf),
            pltpu.SemaphoreType.DMA,
            pltpu.SemaphoreType.DMA((6,)),
            pltpu.SemaphoreType.DMA((2,)),
            pltpu.SemaphoreType.DMA((2,)),
            pltpu.SemaphoreType.DMA((2,)),
            pltpu.SemaphoreType.DMA((2,)),
            pltpu.SemaphoreType.DMA((2, rows)),
            pltpu.SemaphoreType.DMA((3, rows)),
            pltpu.SemaphoreType.DMA((4, rows)),
        ],
        compiler_params=pltpu.CompilerParams(collective_id=0, has_side_effects=True),
    )(block_ids, video, conv_weight.reshape(3, 3, 3 * chans, chans), w_query, w_key, w_value)
    mixed = hidden.astype(jnp.float32).reshape(-1, chans) + jnp.dot(
        attended.reshape(-1, chans), w_output, preferred_element_type=jnp.float32)
    return mixed.astype(bf).reshape(video.shape)


def solution(mesh):
    placed = (P(("groups", "tm"), "height", None, None), P("groups"), P(), P(), P(), P(), P())
    return jax.shard_map(
        per_device,
        mesh=mesh,
        in_specs=placed,
        out_specs=P(("groups", "tm"), "height", None, None),
        check_vma=False,
    )
```

```python
import functools

import jax
import jax.numpy as jnp
from jax import lax
from jax.experimental import pallas as pl
from jax.experimental.pallas import tpu as pltpu
from jax.sharding import PartitionSpec as P

HD = 64
REACH = 7
MESH = pl.DeviceIdType.MESH


def normalize(wide):
    return wide * lax.rsqrt(jnp.mean(wide * wide, axis=-1, keepdims=True) + 1e-06)


def kernel(n, ids, video, conv_w, w_q, w_k, w_v, out, held,
           raw, act, cw, pw, acc, nb, qs, ks, vs, place, spread,
           load_sem, weight_sem, row_send, row_recv, halo_send, halo_recv,
           own_send, fwd_send, nb_recv):
    count, rows, cols, chans = video.shape
    me = lax.axis_index("tm")
    core = lax.axis_index("height")
    even = lax.rem(me, 2) == 0
    odd = lax.rem(me, 2) == 1

    def peer(by):
        return {"tm": me + by}

    other = {"height": 1 - core}

    own_load = pltpu.make_async_copy(video, raw.at[2:4, 1:rows + 1], load_sem)
    own_load.start()
    w_loads = {}
    for a in (2, 1, 0):
        w_loads[a] = pltpu.make_async_copy(conv_w.at[a], cw.at[a], weight_sem.at[a])
        w_loads[a].start()
    p_loads = []
    for j, w in enumerate((w_q, w_k, w_v)):
        p_loads.append(pltpu.make_async_copy(w, pw.at[j], weight_sem.at[3 + j]))
        p_loads[-1].start()

    barrier = pltpu.get_barrier_semaphore()
    near = [(me >= 1, -1), (me <= n - 2, 1), (me >= 2, -2), (me <= n - 3, 2)]
    pl.semaphore_signal(barrier, inc=1, device_id=other, device_id_type=MESH)
    for cond, by in near:
        @pl.when(cond)
        def _(by=by):
            pl.semaphore_signal(barrier, inc=1, device_id=peer(by), device_id_type=MESH)

    blank = jnp.zeros((cols, chans), jnp.bfloat16)
    outer = (rows + 1) * core
    inner = (rows + 1) * (1 - core)
    for e in range(4):
        raw[e, outer] = blank

    @pl.when(me == 0)
    def _():
        for e in range(2):
            for r in range(rows + 2):
                raw[e, r] = blank

    for d in range(1, 5):
        @pl.when(me < d)
        def _(d=d):
            for f in range(2):
                nb[8 - 2 * d + f] = jnp.zeros((rows, cols, chans), jnp.bfloat16)

    for at in (0, 1, n - 2, n - 1):
        @pl.when(me == at)
        def _(at=at):
            pl.semaphore_wait(barrier, 1 + sum(0 <= at + by < n for by in (-2, -1, 1, 2)))

    @pl.when((me >= 2) & (me <= n - 3))
    def _():
        pl.semaphore_wait(barrier, 5)

    edge = (rows - 1) * (1 - core)
    landing = (rows + 1) * core
    half = rows // 2

    def halo(part):
        start, size = ((core, rows - 1), (edge, 1))[part]
        return pltpu.make_async_remote_copy(
            src_ref=video.at[:, pl.ds(start, size)],
            dst_ref=raw.at[0:2, pl.ds(1 + start, size)],
            send_sem=halo_send.at[part], recv_sem=halo_recv.at[part],
            device_id=peer(1), device_id_type=MESH)

    def row(e):
        src = video.at[:, edge] if e else raw.at[0:2, 1 + edge]
        return pltpu.make_async_remote_copy(
            src_ref=src, dst_ref=raw.at[2 * e:2 * e + 2, landing],
            send_sem=row_send.at[e], recv_sem=row_recv.at[e],
            device_id=other, device_id_type=MESH)

    @pl.when(me <= n - 2)
    def _():
        halo(0).start()
        halo(1).start()

    row(1).start()

    col = lax.broadcasted_iota(jnp.int32, (cols, chans), 0)

    def activate(e, r):
        v = normalize(raw[e, r].astype(jnp.float32))
        v = v / (1.0 + jnp.exp(-v))
        act[e, r, :, chans:2 * chans] = v.astype(jnp.bfloat16)
        left = jnp.where(col == 0, 0.0, pltpu.roll(v, 1, 0))
        right = jnp.where(col == cols - 1, 0.0, pltpu.roll(v, cols - 1, 0))
        act[e, r, :, 0:chans] = left.astype(jnp.bfloat16)
        act[e, r, :, 2 * chans:3 * chans] = right.astype(jnp.bfloat16)

    def activate_rows(e0, start, size):
        for e in (e0, e0 + 1):
            for r in range(size):
                activate(e, start + r)

    empty = jnp.zeros((cols, 3 * chans), jnp.bfloat16)
    for e in range(4):
        act[e, outer] = empty

    def taps(p, a):
        base = half * (p + core * (1 - 2 * p))
        total = None
        for b in range(3):
            window = act[a:a + 2, pl.ds(base + b, half)].reshape(2 * half * cols, 3 * chans)
            term = jnp.dot(window, cw[a, b], preferred_element_type=jnp.float32)
            total = term if total is None else total + term
        return total

    own_load.wait()
    activate_rows(2, 1, rows)
    w_loads[2].wait()
    acc[0] = taps(0, 2)
    row(1).wait()
    activate_rows(2, inner, 1)
    acc[1] = taps(1, 2)
    w_loads[1].wait()
    w_loads[0].wait()

    def line(p):
        return p + core * (rows - 1 - 2 * p)

    def copy_to(src, dst, size, p, by, send_sem, recv_sem):
        return pltpu.make_async_remote_copy(
            src_ref=nb.at[src:src + size, line(p)], dst_ref=nb.at[dst:dst + size, line(p)],
            send_sem=send_sem, recv_sem=recv_sem,
            device_id=peer(by), device_id_type=MESH)

    def own_next(p):
        return copy_to(8, 6, 2, p, 1, own_send.at[0, p], nb_recv.at[0, p])

    def own_skip(p):
        return copy_to(8, 4, 2, p, 2, own_send.at[1, p], nb_recv.at[1, p])

    def fwd_side_even(p):
        return copy_to(4, 2, 2, p, 1, fwd_send.at[0, p], nb_recv.at[2, p])

    def fwd_side_odd(p):
        return copy_to(4, 6, 2, p, -1, fwd_send.at[0, p], nb_recv.at[0, p])

    def fwd_skip_even(p):
        return copy_to(5, 1, 1, p, 2, fwd_send.at[1, p], nb_recv.at[3, p])

    def fwd_skip_odd(p):
        return copy_to(4, 0, 2, p, 2, fwd_send.at[1, p], nb_recv.at[3, p])

    def fwd_far_odd(p):
        return copy_to(0, 2, 2, p, -1, fwd_send.at[2, p], nb_recv.at[2, p])

    def first_line(p):
        return half * (p + core * (1 - 2 * p))

    def finish(p):
        at = pl.ds(first_line(p), half)
        mixed = raw[2:4, pl.ds(first_line(p) + 1, half)].astype(jnp.float32)
        mixed = mixed + acc[p].reshape(mixed.shape)
        hidden = mixed.astype(jnp.bfloat16)
        held[:, at] = hidden
        nb[8:10, at] = normalize(hidden.astype(jnp.float32)).astype(jnp.bfloat16)
        for k in range(half):
            @pl.when(me <= n - 3)
            def _(k=k):
                own_skip(half * p + k).start()

            @pl.when(even)
            def _(k=k):
                own_next(half * p + k).start()

    c0 = lax.broadcasted_iota(jnp.int32, (chans, 128), 0) // HD
    l0 = lax.broadcasted_iota(jnp.int32, (chans, 128), 1)
    c1 = lax.broadcasted_iota(jnp.int32, (128, chans), 1) // HD
    l1 = lax.broadcasted_iota(jnp.int32, (128, chans), 0)
    for f in range(2):
        for s in range(f, f + 8):
            place[f * 8 + s - f] = jnp.where(
                l0 == c0 + (s * 8 + f * 4), HD ** (-0.5), 0.0).astype(jnp.bfloat16)
            spread[f * 8 + s - f] = jnp.where(
                l1 == c1 + (s * 8 + f * 4), 1.0, 0.0).astype(jnp.bfloat16)

    @pl.when(me >= 1)
    def _():
        halo(0).wait_recv()
    activate_rows(0, 1 + core, rows - 1)
    acc[0] += taps(0, 1) + taps(0, 0)
    finish(0)

    @pl.when(me >= 1)
    def _():
        halo(1).wait_recv()
        row(0).start()
    activate_rows(0, 1 + edge, 1)

    @pl.when(me >= 1)
    def _():
        row(0).wait()
    activate_rows(0, inner, 1)
    acc[1] += taps(1, 1) + taps(1, 0)
    finish(1)

    for load in p_loads:
        load.wait()

    def project(x, j):
        return jnp.dot(x, pw[j], preferred_element_type=jnp.float32).astype(jnp.bfloat16)

    def keyed(idx, size, p):
        at = pl.ds(first_line(p), half)
        shape = (size, half, cols, chans)
        x = nb[idx:idx + size, at].reshape(size * half * cols, chans)
        ks[idx:idx + size, at] = project(x, 1).reshape(shape)
        vs[idx:idx + size, at] = project(x, 2).reshape(shape)

    def own(p):
        at = pl.ds(first_line(p), half)
        x = nb[8:10, at].reshape(2 * half * cols, chans)
        qs[:, at] = project(x, 0).reshape(2, half, cols, chans)
        keyed(8, 2, p)

    def relay_near(p):
        @pl.when(even & (me >= 2))
        def _():
            own_skip(p).wait_recv()
            fwd_side_even(p).start()

        @pl.when(even & (me >= 2) & (me <= n - 3))
        def _():
            fwd_skip_even(p).start()

        @pl.when(odd & (me >= 2))
        def _():
            own_skip(p).wait_recv()
            fwd_side_odd(p).start()

        @pl.when(odd & (me >= 2) & (me <= n - 3))
        def _():
            fwd_skip_odd(p).start()

    def relay_far(p):
        @pl.when(odd & (me >= 4))
        def _():
            fwd_skip_odd(p).wait_recv()
            fwd_far_odd(p).start()

        @pl.when(even & (me >= 4))
        def _():
            fwd_skip_even(p).wait_recv()

    frames = ids.shape[0]
    lane = lax.broadcasted_iota(jnp.int32, (1, 128), 1)
    slot = lane // 8
    which = lax.rem(lane, 8) // 4
    first = me * 2
    key_id = jnp.zeros((1, 128), jnp.int32)
    for s in range(9):
        key_id = jnp.where(slot == s, ids[lax.rem(first - REACH + s + frames, frames)], key_id)
    query_id = jnp.where(which == 0, ids[first], ids[first + 1])
    key_frame = first - REACH + slot
    allowed = ((slot < 9) & (key_frame >= 0) & (key_frame <= first + which)
               & (slot >= which) & (slot < which + 8) & (key_id >= query_id - 1))

    def attend(p):
        at = pl.ds(first_line(p), half)
        group = half * cols

        def part(ref, idx):
            return ref[idx, at].reshape(group, chans).astype(jnp.float32)

        scores = jnp.zeros((group, 128), jnp.float32)
        for f in range(2):
            query = part(qs, f)
            for j in range(8):
                prod = query * part(ks, 1 + f + j)
                high = prod.astype(jnp.bfloat16)
                low = (prod - high.astype(jnp.float32)).astype(jnp.bfloat16)
                spot = place[f * 8 + j]
                scores = scores + jnp.dot(high, spot, preferred_element_type=jnp.float32)
                scores = scores + jnp.dot(low, spot, preferred_element_type=jnp.float32)
        scores = jnp.where(allowed, scores, -1e30)
        top = scores
        for by in (64, 32, 16, 8):
            top = jnp.maximum(top, pltpu.roll(top, by, 1))
        expo = jnp.exp(scores - top)
        total = expo
        for by in (64, 32, 16, 8):
            total = total + pltpu.roll(total, by, 1)
        weights = (expo / total).astype(jnp.bfloat16)
        for f in range(2):
            got = jnp.zeros((group, chans), jnp.float32)
            for j in range(8):
                wide = jnp.dot(weights, spread[f * 8 + j], preferred_element_type=jnp.float32)
                got = got + wide * part(vs, 1 + f + j)
            out[f, at] = got.astype(jnp.bfloat16).reshape(half, cols, chans)

    def take(d, p):
        sem = nb_recv.at[{1: 0, 3: 2}[d], p]

        @pl.when(me >= d)
        def _():
            copy_to(8 - 2 * d, 8 - 2 * d, 2, p, 1, own_send.at[0, 0], sem).wait_recv()

    halves = (range(half), range(half, rows))
    for h in range(2):
        for p in halves[h]:
            relay_near(p)
        own(h)
    keyed(4, 2, 0)
    for p in halves[0]:
        relay_far(p)
    keyed(4, 2, 1)
    keyed(1, 1, 0)
    for p in halves[0]:
        take(1, p)
    keyed(6, 2, 0)
    for p in halves[1]:
        relay_far(p)
    keyed(1, 1, 1)
    for p in halves[0]:
        take(3, p)
    keyed(2, 2, 0)
    attend(0)
    for p in halves[1]:
        take(1, p)
        take(3, p)
    keyed(6, 2, 1)
    keyed(2, 2, 1)
    attend(1)

    @pl.when(me <= n - 2)
    def _():
        halo(0).wait_send()
        halo(1).wait_send()

    for p in range(rows):
        @pl.when(me <= n - 3)
        def _(p=p):
            own_skip(p).wait_send()

        @pl.when(even)
        def _(p=p):
            own_next(p).wait_send()

        @pl.when(me >= 2)
        def _(p=p):
            fwd_side_even(p).wait_send()

        @pl.when(even & (me >= 2) & (me <= n - 3))
        def _(p=p):
            fwd_skip_even(p).wait_send()

        @pl.when(odd & (me >= 2) & (me <= n - 3))
        def _(p=p):
            fwd_skip_odd(p).wait_send()

        @pl.when(odd & (me >= 4))
        def _(p=p):
            fwd_far_odd(p).wait_send()


def per_device(video, block_ids, conv_weight, w_query, w_key, w_value, w_output):
    count, rows, cols, chans = video.shape
    n = lax.axis_size("tm")
    assert count == 2 and n % 2 == 0 and n >= 4 and lax.axis_size("height") == 2
    assert rows % 2 == 0
    group = rows * cols
    bf = jnp.bfloat16
    anywhere = pl.BlockSpec(memory_space=pl.ANY)
    attended, hidden = pl.pallas_call(
        functools.partial(kernel, n),
        out_shape=[jax.ShapeDtypeStruct(video.shape, bf)] * 2,
        in_specs=[pl.BlockSpec(memory_space=pltpu.SMEM)] + [anywhere] * 5,
        out_specs=[pl.BlockSpec(memory_space=pltpu.VMEM)] * 2,
        scratch_shapes=[
            pltpu.VMEM((4, rows + 2, cols, chans), bf),
            pltpu.VMEM((4, rows + 2, cols, 3 * chans), bf),
            pltpu.VMEM((3, 3, 3 * chans, chans), bf),
            pltpu.VMEM((3, chans, chans), bf),
            pltpu.VMEM((2, group, chans), jnp.float32),
            pltpu.VMEM((10, rows, cols, chans), bf),
            pltpu.VMEM((2, rows, cols, chans), bf),
            pltpu.VMEM((10, rows, cols, chans), bf),
            pltpu.VMEM((10, rows, cols, chans), bf),
            pltpu.VMEM((16, chans, 128), bf),
            pltpu.VMEM((16, 128, chans), bf),
            pltpu.SemaphoreType.DMA,
            pltpu.SemaphoreType.DMA((6,)),
            pltpu.SemaphoreType.DMA((2,)),
            pltpu.SemaphoreType.DMA((2,)),
            pltpu.SemaphoreType.DMA((2,)),
            pltpu.SemaphoreType.DMA((2,)),
            pltpu.SemaphoreType.DMA((2, rows)),
            pltpu.SemaphoreType.DMA((3, rows)),
            pltpu.SemaphoreType.DMA((4, rows)),
        ],
        compiler_params=pltpu.CompilerParams(collective_id=0, has_side_effects=True),
    )(block_ids, video, conv_weight.reshape(3, 3, 3 * chans, chans), w_query, w_key, w_value)
    mixed = hidden.astype(jnp.float32).reshape(-1, chans) + jnp.dot(
        attended.reshape(-1, chans), w_output, preferred_element_type=jnp.float32)
    return mixed.astype(bf).reshape(video.shape)


def solution(mesh):
    placed = (P(("groups", "tm"), "height", None, None), P("groups"), P(), P(), P(), P(), P())
    return jax.shard_map(
        per_device,
        mesh=mesh,
        in_specs=placed,
        out_specs=P(("groups", "tm"), "height", None, None),
        check_vma=False,
    )
```
